256 devices in a mesh: ctx: 32 (over z, y_hi, core), head: 8 (over x, y_lo).
Axes of the slice: x: 4, y: 4 (y_hi: 2, y_lo: 2; y = y_hi * 2 + y_lo), z: 8, core: 2. Of those that a mesh axis runs over, the one named last changes fastest.
Arguments:
- response_input: bfloat16 [512, 8192], P(('ctx', 'head')), may hold values from -6 to 6
- response_queries: bfloat16 [512, 8192], P(('ctx', 'head')), may hold values from -12 to 12
- response_keys: bfloat16 [512, 8192], P(('ctx', 'head')), may hold values from -6 to 6
- response_values: bfloat16 [512, 8192], P(('ctx', 'head')), may hold values from -6 to 6
- prompt_keys: bfloat16 [49152, 8192], P('ctx', 'head'), may hold values from -6 to 6
- prompt_values: bfloat16 [49152, 8192], P('ctx', 'head'), may hold values from -6 to 6
- query_down_weight: bfloat16 [8192, 16], replicated, may hold values from -0.0625 to 0.0625
- query_up_weight: bfloat16 [16, 8192], replicated, may hold values from -1.5 to 1.5
- value_down_weight: bfloat16 [8192, 16], replicated, may hold values from -0.0625 to 0.0625
- value_up_weight: bfloat16 [16, 8192], replicated, may hold values from -1.5 to 1.5
- response_index: int32 [512], replicated, may hold values from 0 to 7, never falling along the last dimension, each value on 1 to 128 neighbouring positions
Outputs:
- out_adapted: bfloat16 [512, 8192], P(('ctx', 'head'))
- out_base: bfloat16 [512, 8192], P(('ctx', 'head'))
The draws below stay inside these ranges and needn't reach their ends.
Inputs may be any that keep to these rules, and one draw needn't show every extreme that they name: `response_index`: never falls along the tokens; each response spans 1 to 128 tokens and one spans exactly 128.
All inputs are finite; a program needn't handle non-finite values.
Results may differ from the reference program's by a relative error of at most 0.0088.
Values may be sent and summed in bfloat16 or wider, within the bound.
No kernel may reach another device: no remote copies, remote signals or barrier semaphores. Data moves between devices by JAX's collectives and lax.ppermute only.
A program may use at most 64 MiB of HBM per device.

```python
import math
import jax
import jax.numpy as jnp
import numpy as np
from jax import lax

HEADS = 64
HD = 128
ADAPTER_RANK = 16
RESPONSES = 8
CACHE_DEV = 1536
MODEL_WIDTH = 8192
QLEN = 512
CACHE = 49152
N_CTX = 32


def draw_response_queries(key, part):
    values = 2.8 * jax.random.truncated_normal(jax.random.fold_in(key, 1), -4.2, 4.2, (QLEN, MODEL_WIDTH), jnp.float32)
    return values.astype(jnp.bfloat16)


def draw_prompt_keys(key, part):
    values = jax.random.truncated_normal(jax.random.fold_in(key, 2), -6.0, 6.0, (CACHE, MODEL_WIDTH), jnp.float32)
    return values.astype(jnp.bfloat16)


def steps_of(key, extent, cuts, smallest, high):
    loudness = 1.0
    for position, shards_of in cuts:
        heights = jax.random.uniform(jax.random.fold_in(jax.random.fold_in(key, 6), position), (shards_of,), jnp.float32, smallest / len(cuts), high / len(cuts))
        loudness = loudness * jnp.repeat(jnp.exp(heights), extent[position] // shards_of).reshape((-1,) + (1,) * (len(extent) - 1 - position))
    return loudness


def length_profile(count, total, reach, skew):
    loads = [(1 << 20) // math.isqrt(standing ** skew) + 1 for standing in range(2, count + 1)]
    spare, given = total - reach - (count - 1), [1] * (count - 1)
    while spare > 0:
        free = [i for i in range(count - 1) if given[i] < reach]
        mass, budget = sum([loads[i] for i in free]), spare
        for i in free:
            more = min(reach - given[i], max(1, budget * loads[i] // mass), spare)
            given[i] = given[i] + more
            spare = spare - more
    return np.array([reach] + given)


def ragged(key, number_of, total, reach, skew):
    if number_of == 2:
        one = jax.random.randint(key, (), max(1, total - reach), min(reach, total - 1) + 1)
        return jnp.stack([one, total - one])
    lengths = jnp.asarray(length_profile(number_of, total, reach, skew), jnp.int32)
    twos = (number_of - 1) // 2
    source_of, sink = lengths[1:1 + 2 * twos:2], lengths[2:2 + 2 * twos:2]
    margin = jnp.minimum(source_of - 1, reach - sink)
    shifted = jax.random.randint(jax.random.fold_in(key, 1), (twos,), 0, 1 << 20) % (margin + 1)
    lengths = lengths.at[1:1 + 2 * twos:2].set(source_of - shifted).at[2:2 + 2 * twos:2].set(sink + shifted)
    return lengths[jax.random.permutation(jax.random.fold_in(key, 2), number_of)]


def centred(rng, dims, deviation, most, pieces=(), kind=jnp.bfloat16):
    gain = steps_of(rng, dims, pieces, -0.22, 0.18) if pieces else 1.0
    entries = jax.random.normal(rng, dims, jnp.float32) * deviation * gain
    return jnp.minimum(jnp.maximum(entries, -most), most).astype(kind)


def setup_inputs(seed: int = 0) -> dict:
    keys = jax.random.split(jax.random.key(seed), 12)
    response_input = centred(keys[0], (QLEN, MODEL_WIDTH), 1.0, 6.0, ((0, 256),))
    response_queries = draw_response_queries(jax.random.fold_in(keys[11], 71), 0)
    response_keys = centred(keys[2], (QLEN, MODEL_WIDTH), 1.0, 6.0, ((0, 256),))
    response_values = centred(keys[3], (QLEN, MODEL_WIDTH), 1.0, 6.0, ((0, 256),))
    prompt_keys = draw_prompt_keys(jax.random.fold_in(keys[11], 71), 0)
    prompt_values = centred(keys[5], (CACHE, MODEL_WIDTH), 1.0, 6.0, ((0, 32), (1, 8)))
    query_down_weight = centred(keys[6], (MODEL_WIDTH, ADAPTER_RANK), MODEL_WIDTH ** -0.5, 0.0625)
    query_up_weight = centred(keys[7], (ADAPTER_RANK, MODEL_WIDTH), ADAPTER_RANK ** -0.5, 1.5)
    value_down_weight = centred(keys[8], (MODEL_WIDTH, ADAPTER_RANK), MODEL_WIDTH ** -0.5, 0.0625)
    value_up_weight = centred(keys[9], (ADAPTER_RANK, MODEL_WIDTH), ADAPTER_RANK ** -0.5, 1.5)
    response_index = jnp.searchsorted(jnp.cumsum(ragged(keys[10], RESPONSES, QLEN, QLEN // 4, 1)), jnp.arange(QLEN), side="right").astype(jnp.int32)
    return dict(response_input=response_input, response_queries=response_queries, response_keys=response_keys, response_values=response_values, prompt_keys=prompt_keys, prompt_values=prompt_values, query_down_weight=query_down_weight, query_up_weight=query_up_weight, value_down_weight=value_down_weight, value_up_weight=value_up_weight, response_index=response_index)


def reference(response_input, response_queries, response_keys, response_values, prompt_keys, prompt_values, query_down_weight, query_up_weight, value_down_weight, value_up_weight, response_index):
    query_lowrank = jnp.dot(response_input, query_down_weight, preferred_element_type=jnp.float32).astype(jnp.bfloat16)
    value_lowrank = jnp.dot(response_input, value_down_weight, preferred_element_type=jnp.float32).astype(jnp.bfloat16)
    query_with_adapter = (response_queries.astype(jnp.float32) + jnp.dot(query_lowrank, query_up_weight, preferred_element_type=jnp.float32)).astype(jnp.bfloat16)
    value_with_adapter = (response_values.astype(jnp.float32) + jnp.dot(value_lowrank, value_up_weight, preferred_element_type=jnp.float32)).astype(jnp.bfloat16)
    queries = jnp.stack([query_with_adapter, response_queries], 1).reshape(QLEN, 2, HEADS, HD)
    stretch_values = jnp.stack([value_with_adapter, response_values], 1)
    shard_len = QLEN // N_CTX
    block_rows = 128 if QLEN % 128 == 0 else QLEN
    scale = HD ** -0.5

    def fold(running, shard_index):
        best, totals, weighted = running
        cache_start = (shard_index * CACHE_DEV).astype(jnp.int32)
        stretch_start = (shard_index * shard_len).astype(jnp.int32)
        key_rows = jnp.concatenate([lax.dynamic_slice_in_dim(prompt_keys, cache_start, CACHE_DEV, 0), lax.dynamic_slice_in_dim(response_keys, stretch_start, shard_len, 0)], 0)
        key_rows = key_rows.reshape(-1, HEADS, HD).astype(jnp.float32)
        cache_part = lax.dynamic_slice_in_dim(prompt_values, cache_start, CACHE_DEV, 0)
        value_rows = jnp.concatenate([jnp.stack([cache_part, cache_part], 1), lax.dynamic_slice_in_dim(stretch_values, stretch_start, shard_len, 0)], 0)
        value_rows = value_rows.reshape(-1, 2, HEADS, HD).astype(jnp.float32)
        key_pos = stretch_start + jnp.arange(shard_len, dtype=jnp.int32)
        key_seg = lax.dynamic_slice_in_dim(response_index, stretch_start, shard_len, 0)

        def one_block(block_index):
            start = (block_index * block_rows).astype(jnp.int32)
            query_block = lax.dynamic_slice_in_dim(queries, start, block_rows, 0).astype(jnp.float32)
            scores = jnp.einsum('qshd,khd->qshk', query_block, key_rows) * scale
            query_pos = start + jnp.arange(block_rows, dtype=jnp.int32)
            query_seg = lax.dynamic_slice_in_dim(response_index, start, block_rows, 0)
            stretch_ok = (key_pos[None, :] <= query_pos[:, None]) & (key_seg[None, :] == query_seg[:, None])
            visible = jnp.concatenate([jnp.ones((block_rows, CACHE_DEV), bool), stretch_ok], 1)
            scores = jnp.where(visible[:, None, None, :], scores, -jnp.inf)
            row_max = jnp.max(scores, -1)
            probs = jnp.exp(scores - row_max[..., None]).astype(jnp.bfloat16).astype(jnp.float32)
            part_total = jnp.sum(probs, -1)
            part_out = jnp.einsum('qshk,kshd->qshd', probs, value_rows)
            part_mean = lax.optimization_barrier((part_out / part_total[..., None]).astype(jnp.bfloat16)).astype(jnp.float32)
            return part_mean, part_total, row_max

        part_mean, part_total, part_max = lax.map(one_block, jnp.arange(QLEN // block_rows, dtype=jnp.int32))
        part_mean = part_mean.reshape(QLEN, 2, HEADS, HD)
        part_total = part_total.reshape(QLEN, 2, HEADS)
        part_max = part_max.reshape(QLEN, 2, HEADS)
        new_best = jnp.maximum(best, part_max)
        old_scale = jnp.exp(best - new_best)
        part_weight = part_total * jnp.exp(part_max - new_best)
        totals = totals * old_scale + part_weight
        weighted = weighted * old_scale[..., None] + part_mean * part_weight[..., None]
        return (new_best, totals, weighted), None

    initial = (jnp.full((QLEN, 2, HEADS), -jnp.inf, jnp.float32), jnp.zeros((QLEN, 2, HEADS), jnp.float32), jnp.zeros((QLEN, 2, HEADS, HD), jnp.float32))
    final, unused = lax.scan(fold, initial, jnp.arange(N_CTX, dtype=jnp.int32))
    result = (final[2] / final[1][..., None]).astype(jnp.bfloat16).reshape(QLEN, 2, HEADS * HD)
    return result[:, 0], result[:, 1]
```

```python
import jax
import jax.numpy as jnp
from jax import lax
from jax.experimental import pallas as pl
from jax.experimental.pallas import tpu as pltpu
from jax.sharding import Mesh, PartitionSpec as P

HD = 128
SCALE = HD**-0.5
LOG2E = 1.4426950408889634
HIDDEN = -1e30
KEY_CHUNK = 256
LAST_DIMS = (((1,), (1,)), ((), ()))
BF16 = jnp.bfloat16
F32 = jnp.float32


def swap(size, flip=1):
    return [(i, i ^ flip) for i in range(size)]


def whole(shape):
    return pl.BlockSpec(shape, lambda: (0,) * len(shape))


def prepare_kernel(x_ref, q_ref, k_ref, v_ref, wq_ref, wv_ref, queries_ref, stretch_ref, fq_ref, fv_ref):
    rank = wq_ref.shape[0]
    width = q_ref.shape[2]
    x = x_ref[...]
    fq_ref[...] = jnp.zeros_like(fq_ref)
    fv_ref[...] = jnp.zeros_like(fv_ref)
    fq_ref[:, :rank] = lax.dot_general(x, wq_ref[...], LAST_DIMS, preferred_element_type=F32)
    fv_ref[:, :rank] = lax.dot_general(x, wv_ref[...], LAST_DIMS, preferred_element_type=F32)
    fq = fq_ref[...].astype(BF16)
    fv = fv_ref[...].astype(BF16)
    for g in range(q_ref.shape[0]):
        q = q_ref[g]
        for part in range(queries_ref.shape[0]):
            queries_ref[part, g, :, :width] = q
            queries_ref[part, g, :, width:] = fq
        stretch_ref[g, :, :width] = k_ref[g]
        stretch_ref[g, :, width : 2 * width] = v_ref[g]
        stretch_ref[g, :, 2 * width :] = fv


def prepare(x, q, k, v, wq, wv, parts):
    groups, rows, width = q.shape
    return pl.pallas_call(
        prepare_kernel,
        out_shape=(
            jax.ShapeDtypeStruct((parts, groups, rows, width + 128), BF16),
            jax.ShapeDtypeStruct((groups, rows, 2 * width + 128), BF16),
        ),
        scratch_shapes=[pltpu.VMEM((rows, 128), F32), pltpu.VMEM((rows, 128), F32)],
        name="prepare",
    )(x, q, k, v, wq, wv)


def pack_lse(lse, lane):
    lse = jnp.where(lane < 8, lse, 0.0)
    high = lse.astype(BF16).astype(F32)
    middle = (lse - high).astype(BF16).astype(F32)
    low = lse - high - middle
    return (high + pltpu.roll(middle, 8, 1) + pltpu.roll(low, 16, 1)).astype(BF16)


def unpack_lse(packed):
    x = packed.astype(F32)
    return x + pltpu.roll(x, 120, 1) + pltpu.roll(x, 112, 1)


def attend_kernel(
    where_ref, own_ref, other_ref, keys_ref, values_ref, stretch_ref, wq_ref, wv_ref, bias_ref,
    own_out_ref, other_out_ref, s0_ref, s1_ref, m0_ref, m1_ref, o_ref, l_ref,
):
    side = where_ref[0]
    core = where_ref[1]
    shards, _, shard_rows, _ = own_ref.shape
    n = shards * shard_rows
    rows = 4 * n
    kn, width = keys_ref.shape
    heads = width // HD
    rank = wq_ref.shape[0]
    scores_refs = (s0_ref, s1_ref)
    max_refs = (m0_ref, m1_ref)
    lane = lax.broadcasted_iota(jnp.int32, (n, 128), 1)
    bias_own = bias_ref[2 * side + core]
    bias_other = bias_ref[2 * side + 1 - core]
    bias = jnp.concatenate([bias_own, bias_other, bias_own, bias_other], 0)

    def tokens(ref, at, size):
        return ref[:, side, :, at : at + size].reshape(n, size)

    factors = jnp.concatenate([tokens(own_ref, width, HD), tokens(other_ref, width, HD)], 0)[:, :rank]
    value_factors = stretch_ref[:, 2 * width : 2 * width + rank]

    def begin(h):
        at = h * HD
        base = jnp.concatenate([tokens(own_ref, at, HD), tokens(other_ref, at, HD)], 0)
        adapted = (
            base.astype(F32) + jnp.dot(factors, wq_ref[:, at : at + HD], preferred_element_type=F32)
        ).astype(BF16)
        q = jnp.concatenate([adapted, base], 0)
        near = lax.dot_general(q, stretch_ref[:, at : at + HD], LAST_DIMS, preferred_element_type=F32) + bias
        max_refs[h % 2][...] = jnp.broadcast_to(jnp.max(near, -1, keepdims=True), (rows, 128))
        return q, near

    def score(h, q, j):
        s = lax.dot_general(
            q, keys_ref[j : j + KEY_CHUNK, h * HD : (h + 1) * HD], LAST_DIMS, preferred_element_type=F32
        )
        scores_refs[h % 2][:, j : j + KEY_CHUNK] = s
        m = max_refs[h % 2][...]
        for c in range(0, KEY_CHUNK, 128):
            m = jnp.maximum(m, s[:, c : c + 128])
        max_refs[h % 2][...] = m

    q, near = begin(0)
    for j in range(0, kn, KEY_CHUNK):
        score(0, q, j)
    lses = [jnp.zeros((n, 128), F32) for _ in range(4)]
    for h in range(heads):
        at = h * HD
        if h + 1 < heads:
            q, near_next = begin(h + 1)
        m = jnp.max(max_refs[h % 2][...], -1, keepdims=True)
        shift = m * (SCALE * LOG2E)
        near_probs = jnp.exp2(near * (SCALE * LOG2E) - shift)
        near_total = jnp.sum(near_probs, -1, keepdims=True)
        near_probs = near_probs.astype(BF16)
        base_values = stretch_ref[:, width + at : width + at + HD]
        adapted_values = (
            base_values.astype(F32) + jnp.dot(value_factors, wv_ref[:, at : at + HD], preferred_element_type=F32)
        ).astype(BF16)
        o_ref[: 2 * n] = jnp.dot(near_probs[: 2 * n], adapted_values, preferred_element_type=F32)
        o_ref[2 * n :] = jnp.dot(near_probs[2 * n :], base_values, preferred_element_type=F32)
        l_ref[...] = jnp.zeros_like(l_ref)
        for j in range(0, kn, KEY_CHUNK):
            if h + 1 < heads:
                score(h + 1, q, j)
            p = jnp.exp2(scores_refs[h % 2][:, j : j + KEY_CHUNK] * (SCALE * LOG2E) - shift)
            total = l_ref[...]
            for c in range(0, KEY_CHUNK, 128):
                total += p[:, c : c + 128]
            l_ref[...] = total
            o_ref[...] += jnp.dot(
                p.astype(BF16), values_ref[j : j + KEY_CHUNK, at : at + HD], preferred_element_type=F32
            )
        total = jnp.sum(l_ref[...], -1, keepdims=True) + near_total
        mean = (o_ref[...] / total).astype(BF16)
        lse = m * SCALE + jnp.log(total)
        for stream in range(2):
            for partner, out_ref in enumerate((own_out_ref, other_out_ref)):
                i = 2 * stream + partner
                out_ref[stream, :, at : at + HD] = mean[i * n : (i + 1) * n]
                lses[i] = jnp.where(lane == h, lse[i * n : (i + 1) * n], lses[i])
        if h + 1 < heads:
            near = near_next
    for stream in range(2):
        own_out_ref[stream, :, width:] = pack_lse(lses[2 * stream], lane)
        other_out_ref[stream, :, width:] = pack_lse(lses[2 * stream + 1], lane)


def attend(where, own, other, keys, values, stretch, wq, wv, bias):
    shards, _, shard_rows, padded = own.shape
    n = shards * shard_rows
    kn, width = keys.shape
    heads = width // HD
    out = jax.ShapeDtypeStruct((2, n, padded), BF16)
    vmem = pl.BlockSpec(memory_space=pltpu.VMEM)
    return pl.pallas_call(
        attend_kernel,
        in_specs=[pl.BlockSpec(memory_space=pltpu.SMEM)] + [vmem] * 8,
        out_specs=[vmem, vmem],
        out_shape=[out, out],
        scratch_shapes=[pltpu.VMEM((4 * n, kn), F32)] * 2 + [pltpu.VMEM((4 * n, 128), F32)] * 4,
        cost_estimate=pl.CostEstimate(
            flops=16 * n * kn * heads * HD, bytes_accessed=4 * kn * width, transcendentals=4 * n * kn * heads
        ),
        compiler_params=pltpu.CompilerParams(vmem_limit_bytes=32 << 20),
        name="attend",
    )(where, own, other, keys, values, stretch, wq, wv, bias)


def merge(pieces, width):
    lane = lax.broadcasted_iota(jnp.int32, (pieces[0].shape[0], 128), 1)
    lses = [unpack_lse(x[:, width:]) for x in pieces]
    best = lses[0]
    for lse in lses[1:]:
        best = jnp.maximum(best, lse)
    weights = [jnp.exp(lse - best) for lse in lses]
    total = weights[0]
    for w in weights[1:]:
        total = total + w
    weights = [w / total for w in weights]
    means = []
    for h in range(width // HD):
        at = h * HD
        mean = weights[0][:, h : h + 1] * pieces[0][:, at : at + HD].astype(F32)
        for w, x in zip(weights[1:], pieces[1:]):
            mean += w[:, h : h + 1] * x[:, at : at + HD].astype(F32)
        means.append(mean.astype(BF16))
    return means, pack_lse(best + jnp.log(total), lane)


def merge_pair_kernel(a_ref, b_ref, out_ref):
    width = out_ref.shape[2] - 128
    for s in range(2):
        means, lse = merge([a_ref[s], b_ref[s]], width)
        for h, mean in enumerate(means):
            out_ref[s, :, h * HD : (h + 1) * HD] = mean
        out_ref[s, :, width:] = lse


def merge_pair(a, b):
    return pl.pallas_call(
        merge_pair_kernel,
        out_shape=jax.ShapeDtypeStruct(a.shape, BF16),
        cost_estimate=pl.CostEstimate(flops=8 * a.size, bytes_accessed=6 * a.size, transcendentals=0),
        name="merge_pair",
    )(a, b)


def merge_send_kernel(a_ref, b_ref, c_ref, out_ref):
    width = out_ref.shape[3] - 128
    for s in range(2):
        means, lse = merge([a_ref[s], b_ref[s], c_ref[s]], width)
        for at, block in enumerate(means + [lse]):
            for p in range(out_ref.shape[0]):
                out_ref[p, s, :, at * HD : (at + 1) * HD] = block[2 * p : 2 * p + 2]


def merge_send(a, b, c):
    _, n, padded = a.shape
    return pl.pallas_call(
        merge_send_kernel,
        out_shape=jax.ShapeDtypeStruct((n // 2, 2, 2, padded), BF16),
        cost_estimate=pl.CostEstimate(flops=12 * a.size, bytes_accessed=8 * a.size, transcendentals=0),
        name="merge_send",
    )(a, b, c)


def finish_kernel(x_ref, a_ref, b_ref):
    parts, groups = x_ref.shape[:2]
    width = a_ref.shape[2]
    for g in range(groups):
        for s, out_ref in enumerate((a_ref, b_ref)):
            lses = [unpack_lse(x_ref[z, g, s, :, width:]) for z in range(parts)]
            best = lses[0]
            for lse in lses[1:]:
                best = jnp.maximum(best, lse)
            weights = [jnp.exp(lse - best) for lse in lses]
            total = weights[0]
            for w in weights[1:]:
                total = total + w
            weights = [w / total for w in weights]
            for h in range(width // HD):
                at = h * HD
                acc = weights[0][:, h : h + 1] * x_ref[0, g, s, :, at : at + HD].astype(F32)
                for z in range(1, parts):
                    acc += weights[z][:, h : h + 1] * x_ref[z, g, s, :, at : at + HD].astype(F32)
                out_ref[g, :, at : at + HD] = acc.astype(BF16)


def finish(x):
    parts, groups, _, rows, padded = x.shape
    out = jax.ShapeDtypeStruct((groups, rows, padded - 128), BF16)
    return pl.pallas_call(finish_kernel, out_shape=(out, out), name="finish")(x)


def local(
    response_input,
    response_queries,
    response_keys,
    response_values,
    prompt_keys,
    prompt_values,
    query_down_weight,
    query_up_weight,
    value_down_weight,
    value_up_weight,
    response_index,
):
    nz, ny, nc = (lax.axis_size(a) for a in ("z", "yh", "c"))
    groups = lax.axis_size("x") * lax.axis_size("yl")
    rows, model = response_queries.shape
    width = model // groups
    shard_rows = rows * groups
    side, core = lax.axis_index("yh"), lax.axis_index("c")
    part = (lax.axis_index("z") * ny + side) * nc + core
    group = lax.axis_index("x") * lax.axis_size("yl") + lax.axis_index("yl")

    def by_group(a):
        return a.reshape(rows, groups, width).transpose(1, 0, 2)

    queries, stretch = prepare(
        response_input,
        by_group(response_queries),
        by_group(response_keys),
        by_group(response_values),
        query_down_weight.T,
        value_down_weight.T,
        nz * ny,
    )
    queries = lax.all_to_all(
        queries.reshape(nz * ny * groups, rows, width + 128), ("z", "yh", "x", "yl"), 0, 0, tiled=True
    )
    stretch = lax.all_to_all(stretch, ("x", "yl"), 0, 0, tiled=True).reshape(shard_rows, 2 * width + 128)
    own = queries.reshape(nz * ny * shard_rows, width + 128)
    other = lax.ppermute(own, "c", swap(nc))
    own = own.reshape(nz, ny, shard_rows, width + 128)
    other = other.reshape(nz, ny, shard_rows, width + 128)

    wq = lax.dynamic_slice_in_dim(query_up_weight, group * width, width, 1)
    wv = lax.dynamic_slice_in_dim(value_up_weight, group * width, width, 1)
    count = response_index.shape[0]
    key_pos = part * shard_rows + jnp.arange(shard_rows, dtype=jnp.int32)
    key_seg = lax.dynamic_slice_in_dim(response_index, part * shard_rows, shard_rows, 0)
    query_pos = jnp.arange(count, dtype=jnp.int32)
    seen = (key_pos[None, :] <= query_pos[:, None]) & (key_seg[None, :] == response_index[:, None])
    bias = jnp.where(seen, 0.0, HIDDEN).astype(F32)
    bias = bias.reshape(nz, ny * nc, shard_rows, shard_rows).transpose(1, 0, 2, 3)
    bias = bias.reshape(ny * nc, nz * shard_rows, shard_rows)

    def attend_side(to):
        where = jnp.stack([to, core]).astype(jnp.int32)
        return attend(where, own, other, prompt_keys, prompt_values, stretch, wq, wv, bias)

    far_own, far_other = attend_side(1 - side)
    far = merge_pair(far_own, lax.ppermute(far_other, "c", swap(nc)))
    far = lax.ppermute(far, "yh", swap(ny))
    near_own, near_other = attend_side(side)
    sends = merge_send(near_own, lax.ppermute(near_other, "c", swap(nc)), far)
    parts = lax.all_to_all(sends, ("z", "x", "yl"), 0, 0, tiled=True)
    outs = finish(parts.reshape(nz, groups, 2, rows, width + 128))
    return tuple(o.transpose(1, 0, 2).reshape(rows, model) for o in outs)


def solution(mesh):
    axes = ("z", "yh", "c", "x", "yl")
    torus = Mesh(mesh.devices.reshape(8, 2, 2, 4, 2), axes)
    tokens = P(axes, None)
    cache = P(axes[:3], axes[3:])
    return jax.shard_map(
        local,
        mesh=torus,
        in_specs=(tokens,) * 4 + (cache,) * 2 + (P(),) * 5,
        out_specs=(tokens, tokens),
        check_vma=False,
    )
```

```python
import jax
import jax.numpy as jnp
from jax import lax
from jax.experimental import pallas as pl
from jax.experimental.pallas import tpu as pltpu
from jax.sharding import Mesh, PartitionSpec as P


HD = 128
SCALE = HD**-0.5
LOG2E = 1.4426950408889634
HIDDEN = -1e30
KEY_CHUNK = 256
LAST_DIMS = (((1,), (1,)), ((), ()))
BF16 = jnp.bfloat16
F32 = jnp.float32


def swap(size, flip=1):
    return [(i, i ^ flip) for i in range(size)]


VMEM = pl.BlockSpec(memory_space=pltpu.VMEM)
HBM = pl.BlockSpec(memory_space=pltpu.HBM)


def small(limit=12):
    return pltpu.CompilerParams(vmem_limit_bytes=limit << 20)


def prepare_kernel(x_ref, q_ref, k_ref, v_ref, wq_ref, wv_ref, out_ref, f_ref):
    rank = wq_ref.shape[0]
    x = x_ref[...]
    f_ref[...] = jnp.zeros_like(f_ref)
    f_ref[0, :, :rank] = lax.dot_general(x, wq_ref[...], LAST_DIMS, preferred_element_type=F32)
    f_ref[1, :, :rank] = lax.dot_general(x, wv_ref[...], LAST_DIMS, preferred_element_type=F32)
    fq = f_ref[0].astype(BF16)
    fv = f_ref[1].astype(BF16)
    for g in range(q_ref.shape[0]):
        at = 0
        for piece in (q_ref[g], fq, k_ref[g], v_ref[g], fv):
            out_ref[g, :, at : at + piece.shape[1]] = piece
            at += piece.shape[1]


def prepare(x, q, k, v, wq, wv):
    groups, rows, width = q.shape
    return pl.pallas_call(
        prepare_kernel,
        out_shape=jax.ShapeDtypeStruct((groups, rows, 3 * width + 256), BF16),
        scratch_shapes=[pltpu.VMEM((2, rows, 128), F32)],
        name="prepare",
    )(x, q, k, v, wq, wv)


def fan_kernel(near_ref, far_ref, out_ref):
    rows, padded = far_ref.shape
    near = near_ref[:, :padded]
    far = far_ref[...]
    for z in range(out_ref.shape[0]):
        out_ref[z, :rows] = near
        out_ref[z, rows:] = far


def fan(near, far, parts):
    rows, padded = far.shape
    return pl.pallas_call(
        fan_kernel,
        out_shape=jax.ShapeDtypeStruct((parts, 2 * rows, padded), BF16),
        name="fan",
    )(near, far)


def pack_lse(lse, lane):
    lse = jnp.where(lane < 8, lse, 0.0)
    high = lse.astype(BF16).astype(F32)
    middle = (lse - high).astype(BF16).astype(F32)
    low = lse - high - middle
    return (high + pltpu.roll(middle, 8, 1) + pltpu.roll(low, 16, 1)).astype(BF16)


def unpack_lse(packed):
    x = packed.astype(F32)
    return x + pltpu.roll(x, 120, 1) + pltpu.roll(x, 112, 1)


def attend_kernel(
    where_ref, own_ref, other_ref, keys_hbm, values_hbm, stretch_ref, wq_ref, wv_ref, bias_ref, after_ref,
    own_out_ref, other_out_ref, keys_ref, values_ref, s0_ref, s1_ref, m0_ref, m1_ref, o_ref, l_ref, sems,
):
    del after_ref
    side = where_ref[0]
    shards, _, shard_rows, _ = own_ref.shape
    n = shards * shard_rows
    rows = 4 * n
    kn, width = keys_ref.shape
    heads = width // HD
    rank = wq_ref.shape[0]
    scores_refs = (s0_ref, s1_ref)
    max_refs = (m0_ref, m1_ref)
    lane = lax.broadcasted_iota(jnp.int32, (n, 128), 1)
    bias_own = bias_ref[where_ref[1]]
    bias_other = bias_ref[where_ref[2]]
    keys_at = width + 128
    values_at = keys_at + width
    factors_at = values_at + width
    bias = jnp.concatenate([bias_own, bias_other, bias_own, bias_other], 0)

    def fetch(i, h):
        src, dst = ((keys_hbm, keys_ref), (values_hbm, values_ref))[i]
        cols = slice(h * HD, (h + 1) * HD)
        return pltpu.make_async_copy(src.at[:, cols], dst.at[:, cols], sems.at[i, h])

    order = [(0, 0), (0, 1), (1, 0)] + [(i, h) for h in range(1, heads) for i, h in ((0, h + 1), (1, h)) if h < heads]
    for i, h in order:
        fetch(i, h).start()

    def tokens(ref, at, size):
        return ref[:, side, :, at : at + size].reshape(n, size)

    factors = jnp.concatenate([tokens(own_ref, width, HD), tokens(other_ref, width, HD)], 0)[:, :rank]
    value_factors = stretch_ref[:, factors_at : factors_at + rank]

    def begin(h):
        at = h * HD
        base = jnp.concatenate([tokens(own_ref, at, HD), tokens(other_ref, at, HD)], 0)
        adapted = (
            base.astype(F32) + jnp.dot(factors, wq_ref[:, at : at + HD], preferred_element_type=F32)
        ).astype(BF16)
        q = jnp.concatenate([adapted, base], 0)
        near = lax.dot_general(q, stretch_ref[:, keys_at + at : keys_at + at + HD], LAST_DIMS, preferred_element_type=F32) + bias
        max_refs[h % 2][...] = jnp.broadcast_to(jnp.max(near, -1, keepdims=True), (rows, 128))
        return q, near

    def score(h, q, j):
        s = lax.dot_general(
            q, keys_ref[j : j + KEY_CHUNK, h * HD : (h + 1) * HD], LAST_DIMS, preferred_element_type=F32
        )
        scores_refs[h % 2][:, j : j + KEY_CHUNK] = s
        m = max_refs[h % 2][...]
        for c in range(0, KEY_CHUNK, 128):
            m = jnp.maximum(m, s[:, c : c + 128])
        max_refs[h % 2][...] = m

    q, near = begin(0)
    fetch(0, 0).wait()
    for j in range(0, kn, KEY_CHUNK):
        score(0, q, j)
    fetch(0, 1).wait()
    fetch(1, 0).wait()
    lses = [jnp.zeros((n, 128), F32) for _ in range(4)]
    for h in range(heads):
        at = h * HD
        if h + 1 < heads:
            q, near_next = begin(h + 1)
        m = jnp.max(max_refs[h % 2][...], -1, keepdims=True)
        shift = m * (SCALE * LOG2E)
        near_probs = jnp.exp2(near * (SCALE * LOG2E) - shift)
        near_total = jnp.sum(near_probs, -1, keepdims=True)
        near_probs = near_probs.astype(BF16)
        base_values = stretch_ref[:, values_at + at : values_at + at + HD]
        adapted_values = (
            base_values.astype(F32) + jnp.dot(value_factors, wv_ref[:, at : at + HD], preferred_element_type=F32)
        ).astype(BF16)
        o_ref[: 2 * n] = jnp.dot(near_probs[: 2 * n], adapted_values, preferred_element_type=F32)
        o_ref[2 * n :] = jnp.dot(near_probs[2 * n :], base_values, preferred_element_type=F32)
        l_ref[...] = jnp.zeros_like(l_ref)
        for j in range(0, kn, KEY_CHUNK):
            if h + 1 < heads:
                score(h + 1, q, j)
            p = jnp.exp2(scores_refs[h % 2][:, j : j + KEY_CHUNK] * (SCALE * LOG2E) - shift)
            total = l_ref[...]
            for c in range(0, KEY_CHUNK, 128):
                total += p[:, c : c + 128]
            l_ref[...] = total
            o_ref[...] += jnp.dot(
                p.astype(BF16), values_ref[j : j + KEY_CHUNK, at : at + HD], preferred_element_type=F32
            )
        total = jnp.sum(l_ref[...], -1, keepdims=True) + near_total
        mean = (o_ref[...] / total).astype(BF16)
        lse = m * SCALE + jnp.log(total)
        for stream in range(2):
            for partner, out_ref in enumerate((own_out_ref, other_out_ref)):
                i = 2 * stream + partner
                out_ref[stream, :, at : at + HD] = mean[i * n : (i + 1) * n]
                lses[i] = jnp.where(lane == h, lse[i * n : (i + 1) * n], lses[i])
        if h + 1 < heads:
            near = near_next
        if h == 0:
            for i, later in order[3:]:
                fetch(i, later).wait()
    for stream in range(2):
        own_out_ref[stream, :, width:] = pack_lse(lses[2 * stream], lane)
        other_out_ref[stream, :, width:] = pack_lse(lses[2 * stream + 1], lane)


def attend(where, own, other, keys, values, stretch, wq, wv, bias, after):
    shards, _, shard_rows, padded = own.shape
    n = shards * shard_rows
    kn, width = keys.shape
    heads = width // HD
    out = jax.ShapeDtypeStruct((2, n, padded), BF16)
    return pl.pallas_call(
        attend_kernel,
        in_specs=[pl.BlockSpec(memory_space=pltpu.SMEM), VMEM, VMEM, HBM, HBM] + [VMEM] * 4 + [HBM],
        out_specs=[VMEM, VMEM],
        out_shape=[out, out],
        scratch_shapes=[pltpu.VMEM((kn, width), BF16)] * 2
        + [pltpu.VMEM((4 * n, kn), F32)] * 2
        + [pltpu.VMEM((4 * n, 128), F32)] * 4
        + [pltpu.SemaphoreType.DMA((2, heads))],
        cost_estimate=pl.CostEstimate(
            flops=16 * n * kn * heads * HD, bytes_accessed=4 * kn * width, transcendentals=4 * n * kn * heads
        ),
        compiler_params=small(51),
        name="attend",
    )(where, own, other, keys, values, stretch, wq, wv, bias, after)


def merge(pieces, width):
    lane = lax.broadcasted_iota(jnp.int32, (pieces[0].shape[0], 128), 1)
    lses = [unpack_lse(x[:, width:]) for x in pieces]
    best = lses[0]
    for lse in lses[1:]:
        best = jnp.maximum(best, lse)
    weights = [jnp.exp(lse - best) for lse in lses]
    total = weights[0]
    for w in weights[1:]:
        total = total + w
    weights = [w / total for w in weights]
    means = []
    for h in range(width // HD):
        at = h * HD
        mean = weights[0][:, h : h + 1] * pieces[0][:, at : at + HD].astype(F32)
        for w, x in zip(weights[1:], pieces[1:]):
            mean += w[:, h : h + 1] * x[:, at : at + HD].astype(F32)
        means.append(mean.astype(BF16))
    return means, pack_lse(best + jnp.log(total), lane)


def merge_pair_kernel(a_ref, b_ref, out_ref):
    width = out_ref.shape[2] - 128
    for s in range(2):
        means, lse = merge([a_ref[s], b_ref[s]], width)
        for h, mean in enumerate(means):
            out_ref[s, :, h * HD : (h + 1) * HD] = mean
        out_ref[s, :, width:] = lse


def merge_pair(a, b):
    return pl.pallas_call(
        merge_pair_kernel,
        in_specs=[VMEM, VMEM],
        out_specs=VMEM,
        compiler_params=small(),
        out_shape=jax.ShapeDtypeStruct(a.shape, BF16),
        cost_estimate=pl.CostEstimate(flops=8 * a.size, bytes_accessed=6 * a.size, transcendentals=0),
        name="merge_pair",
    )(a, b)


def merge_send_kernel(a_ref, b_ref, c_ref, out_ref):
    width = out_ref.shape[3] - 128
    for s in range(2):
        means, lse = merge([a_ref[s], b_ref[s], c_ref[s]], width)
        for at, block in enumerate(means + [lse]):
            for p in range(out_ref.shape[0]):
                out_ref[p, s, :, at * HD : (at + 1) * HD] = block[2 * p : 2 * p + 2]


def merge_send(a, b, c):
    _, n, padded = a.shape
    return pl.pallas_call(
        merge_send_kernel,
        in_specs=[VMEM, VMEM, VMEM],
        out_specs=VMEM,
        compiler_params=small(),
        out_shape=jax.ShapeDtypeStruct((n // 2, 2, 2, padded), BF16),
        cost_estimate=pl.CostEstimate(flops=12 * a.size, bytes_accessed=8 * a.size, transcendentals=0),
        name="merge_send",
    )(a, b, c)


def finish_kernel(x_ref, a_ref, b_ref):
    parts = x_ref.shape[0]
    groups, rows, width = a_ref.shape
    means, _ = merge([x_ref[z] for z in range(parts)], width)
    for h, mean in enumerate(means):
        for g in range(groups):
            at = 2 * rows * g
            a_ref[g, :, h * HD : (h + 1) * HD] = mean[at : at + rows]
            b_ref[g, :, h * HD : (h + 1) * HD] = mean[at + rows : at + 2 * rows]


def finish(x, groups, rows):
    out = jax.ShapeDtypeStruct((groups, rows, x.shape[2] - 128), BF16)
    return pl.pallas_call(
        finish_kernel, in_specs=[VMEM], out_specs=[VMEM, VMEM], out_shape=(out, out), compiler_params=small(), name="finish"
    )(x)


def local(
    response_input,
    response_queries,
    response_keys,
    response_values,
    prompt_keys,
    prompt_values,
    query_down_weight,
    query_up_weight,
    value_down_weight,
    value_up_weight,
    response_index,
):
    nz, ny, nc = (lax.axis_size(a) for a in ("z", "yh", "c"))
    groups = lax.axis_size("x") * lax.axis_size("yl")
    rows, model = response_queries.shape
    width = model // groups
    shard_rows = rows * groups
    side, core = lax.axis_index("yh"), lax.axis_index("c")
    part = (lax.axis_index("z") * ny + side) * nc + core
    group = lax.axis_index("x") * lax.axis_size("yl") + lax.axis_index("yl")

    def by_group(a):
        return a.reshape(rows, groups, width).transpose(1, 0, 2)

    padded = width + 128
    sent = prepare(
        response_input,
        by_group(response_queries),
        by_group(response_keys),
        by_group(response_values),
        query_down_weight.T,
        value_down_weight.T,
    )
    stretch = lax.all_to_all(sent, ("x", "yl"), 0, 0, tiled=True).reshape(shard_rows, 3 * width + 256)
    far_rows = lax.ppermute(stretch[:, :padded], "yh", swap(ny))
    own = lax.all_to_all(fan(stretch, far_rows, nz), "z", 0, 0, tiled=True)
    other = lax.ppermute(own, "c", swap(nc))
    own = own.reshape(nz, ny, shard_rows, padded)
    other = other.reshape(nz, ny, shard_rows, padded)

    wq = lax.dynamic_slice_in_dim(query_up_weight, group * width, width, 1)
    wv = lax.dynamic_slice_in_dim(value_up_weight, group * width, width, 1)
    count = response_index.shape[0]
    key_pos = part * shard_rows + jnp.arange(shard_rows, dtype=jnp.int32)
    key_seg = lax.dynamic_slice_in_dim(response_index, part * shard_rows, shard_rows, 0)
    query_pos = jnp.arange(count, dtype=jnp.int32)
    seen = (key_pos[None, :] <= query_pos[:, None]) & (key_seg[None, :] == response_index[:, None])
    bias = jnp.where(seen, 0.0, HIDDEN).astype(F32)
    bias = bias.reshape(nz, ny * nc, shard_rows, shard_rows).transpose(1, 0, 2, 3)
    bias = bias.reshape(ny * nc, nz * shard_rows, shard_rows)

    def attend_side(far, after):
        half = 2 * (side ^ far)
        where = jnp.stack([jnp.int32(far), half + core, half + 1 - core]).astype(jnp.int32)
        return attend(where, own, other, prompt_keys, prompt_values, stretch, wq, wv, bias, after)

    far_own, far_other = attend_side(1, own.reshape(2, nz * shard_rows, padded))
    far = merge_pair(far_own, lax.ppermute(far_other, "c", swap(nc)))
    crossed = lax.ppermute(far, "yh", swap(ny))
    near_own, near_other = attend_side(0, far)
    sends = merge_send(near_own, lax.ppermute(near_other, "c", swap(nc)), crossed)
    parts = lax.all_to_all(sends, ("z", "x", "yl"), 0, 0, tiled=True)
    outs = finish(parts.reshape(nz, groups * 2 * rows, padded), groups, rows)
    return tuple(o.transpose(1, 0, 2).reshape(rows, model) for o in outs)


def solution(mesh):
    axes = ("z", "yh", "c", "x", "yl")
    torus = Mesh(mesh.devices.reshape(8, 2, 2, 4, 2), axes)
    tokens = P(axes, None)
    cache = P(axes[:3], axes[3:])
    return jax.shard_map(
        local,
        mesh=torus,
        in_specs=(tokens,) * 4 + (cache,) * 2 + (P(),) * 5,
        out_specs=(tokens, tokens),
        check_vma=False,
    )
```

```python
import jax
import jax.numpy as jnp
from jax import lax
from jax.experimental import pallas as pl
from jax.experimental.pallas import tpu as pltpu
from jax.sharding import Mesh, PartitionSpec as P


HD = 128
SCALE = HD**-0.5
LOG2E = 1.4426950408889634
HIDDEN = -1e30
KEY_CHUNK = 256
LAST_DIMS = (((1,), (1,)), ((), ()))
BF16 = jnp.bfloat16
F32 = jnp.float32


def swap(size, flip=1):
    return [(i, i ^ flip) for i in range(size)]


VMEM = pl.BlockSpec(memory_space=pltpu.VMEM)
HBM = pl.BlockSpec(memory_space=pltpu.HBM)


def small(limit=12):
    return pltpu.CompilerParams(vmem_limit_bytes=limit << 20)


def prepare_kernel(x_ref, q_ref, k_ref, v_ref, wq_ref, wv_ref, out_ref, f_ref):
    rank = wq_ref.shape[0]
    x = x_ref[...]
    f_ref[...] = jnp.zeros_like(f_ref)
    f_ref[0, :, :rank] = lax.dot_general(x, wq_ref[...], LAST_DIMS, preferred_element_type=F32)
    f_ref[1, :, :rank] = lax.dot_general(x, wv_ref[...], LAST_DIMS, preferred_element_type=F32)
    fq = f_ref[0].astype(BF16)
    fv = f_ref[1].astype(BF16)
    for g in range(q_ref.shape[0]):
        at = 0
        for piece in (q_ref[g], fq, k_ref[g], v_ref[g], fv):
            for half in range(out_ref.shape[0]):
                out_ref[half, g, :, at : at + piece.shape[1]] = piece
            at += piece.shape[1]


def prepare(x, q, k, v, wq, wv, halves):
    groups, rows, width = q.shape
    return pl.pallas_call(
        prepare_kernel,
        out_shape=jax.ShapeDtypeStruct((halves, groups, rows, 3 * width + 256), BF16),
        scratch_shapes=[pltpu.VMEM((2, rows, 128), F32)],
        name="prepare",
    )(x, q, k, v, wq, wv)


def fan_kernel(rows_ref, out_ref):
    rows = rows_ref[...]
    for z in range(out_ref.shape[0]):
        out_ref[z] = rows


def fan(rows, parts, padded):
    count = rows.shape[0]
    return pl.pallas_call(
        fan_kernel,
        grid=(1,),
        in_specs=[pl.BlockSpec((count, padded), lambda i: (0, 0))],
        out_specs=pl.BlockSpec((parts, count, padded), lambda i: (0, 0, 0)),
        out_shape=jax.ShapeDtypeStruct((parts, count, padded), BF16),
        name="fan",
    )(rows)


def pack_lse(lse, lane):
    lse = jnp.where(lane < 8, lse, 0.0)
    high = lse.astype(BF16).astype(F32)
    middle = (lse - high).astype(BF16).astype(F32)
    low = lse - high - middle
    return (high + pltpu.roll(middle, 8, 1) + pltpu.roll(low, 16, 1)).astype(BF16)


def unpack_lse(packed):
    x = packed.astype(F32)
    return x + pltpu.roll(x, 120, 1) + pltpu.roll(x, 112, 1)


def attend_kernel(
    where_ref, own_ref, other_ref, keys_hbm, values_hbm, stretch_ref, wq_ref, wv_ref, bias_ref, after_ref,
    own_out_ref, other_out_ref, keys_ref, values_ref, s0_ref, s1_ref, m0_ref, m1_ref, o_ref, l_ref, sems,
):
    del after_ref
    side = where_ref[0]
    shards, _, shard_rows, _ = own_ref.shape
    n = shards * shard_rows
    rows = 4 * n
    kn, width = keys_ref.shape
    heads = width // HD
    rank = wq_ref.shape[0]
    scores_refs = (s0_ref, s1_ref)
    max_refs = (m0_ref, m1_ref)
    lane = lax.broadcasted_iota(jnp.int32, (n, 128), 1)
    bias_own = bias_ref[where_ref[1]]
    bias_other = bias_ref[where_ref[2]]
    keys_at = width + 128
    values_at = keys_at + width
    factors_at = values_at + width
    bias = jnp.concatenate([bias_own, bias_other, bias_own, bias_other], 0)

    def fetch(i, h):
        src, dst = ((keys_hbm, keys_ref), (values_hbm, values_ref))[i]
        cols = slice(h * HD, (h + 1) * HD)
        return pltpu.make_async_copy(src.at[:, cols], dst.at[:, cols], sems.at[i, h])

    order = [(0, 0), (0, 1), (1, 0)] + [(i, h) for h in range(1, heads) for i, h in ((0, h + 1), (1, h)) if h < heads]
    for i, h in order:
        fetch(i, h).start()

    def tokens(ref, at, size):
        return ref[:, side, :, at : at + size].reshape(n, size)

    factors = jnp.concatenate([tokens(own_ref, width, HD), tokens(other_ref, width, HD)], 0)[:, :rank]
    home = where_ref[3]
    value_factors = stretch_ref[home, :, factors_at : factors_at + rank]

    def begin(h):
        at = h * HD
        base = jnp.concatenate([tokens(own_ref, at, HD), tokens(other_ref, at, HD)], 0)
        adapted = (
            base.astype(F32) + jnp.dot(factors, wq_ref[:, at : at + HD], preferred_element_type=F32)
        ).astype(BF16)
        q = jnp.concatenate([adapted, base], 0)
        near = lax.dot_general(q, stretch_ref[home, :, keys_at + at : keys_at + at + HD], LAST_DIMS, preferred_element_type=F32) + bias
        max_refs[h % 2][...] = jnp.broadcast_to(jnp.max(near, -1, keepdims=True), (rows, 128))
        return q, near

    def score(h, q, j):
        s = lax.dot_general(
            q, keys_ref[j : j + KEY_CHUNK, h * HD : (h + 1) * HD], LAST_DIMS, preferred_element_type=F32
        )
        scores_refs[h % 2][:, j : j + KEY_CHUNK] = s
        m = max_refs[h % 2][...]
        for c in range(0, KEY_CHUNK, 128):
            m = jnp.maximum(m, s[:, c : c + 128])
        max_refs[h % 2][...] = m

    q, near = begin(0)
    fetch(0, 0).wait()
    for j in range(0, kn, KEY_CHUNK):
        score(0, q, j)
    fetch(0, 1).wait()
    fetch(1, 0).wait()
    lses = [jnp.zeros((n, 128), F32) for _ in range(4)]
    for h in range(heads):
        at = h * HD
        if h + 1 < heads:
            q, near_next = begin(h + 1)
        m = jnp.max(max_refs[h % 2][...], -1, keepdims=True)
        near_probs = jnp.exp2((near - m) * (SCALE * LOG2E))
        near_total = jnp.sum(near_probs, -1, keepdims=True)
        near_probs = near_probs.astype(BF16)
        base_values = stretch_ref[home, :, values_at + at : values_at + at + HD]
        adapted_values = (
            base_values.astype(F32) + jnp.dot(value_factors, wv_ref[:, at : at + HD], preferred_element_type=F32)
        ).astype(BF16)
        o_ref[: 2 * n] = jnp.dot(near_probs[: 2 * n], adapted_values, preferred_element_type=F32)
        o_ref[2 * n :] = jnp.dot(near_probs[2 * n :], base_values, preferred_element_type=F32)
        l_ref[...] = jnp.zeros_like(l_ref)
        for j in range(0, kn, KEY_CHUNK):
            if h + 1 < heads:
                score(h + 1, q, j)
            p = jnp.exp2((scores_refs[h % 2][:, j : j + KEY_CHUNK] - m) * (SCALE * LOG2E))
            total = l_ref[...]
            for c in range(0, KEY_CHUNK, 128):
                total += p[:, c : c + 128]
            l_ref[...] = total
            o_ref[...] += jnp.dot(
                p.astype(BF16), values_ref[j : j + KEY_CHUNK, at : at + HD], preferred_element_type=F32
            )
        total = jnp.sum(l_ref[...], -1, keepdims=True) + near_total
        mean = (o_ref[...] / total).astype(BF16)
        lse = m * SCALE + jnp.log(total)
        for stream in range(2):
            for partner, out_ref in enumerate((own_out_ref, other_out_ref)):
                i = 2 * stream + partner
                out_ref[stream, :, at : at + HD] = mean[i * n : (i + 1) * n]
                lses[i] = jnp.where(lane == h, lse[i * n : (i + 1) * n], lses[i])
        if h + 1 < heads:
            near = near_next
        if h == 0:
            for i, later in order[3:]:
                fetch(i, later).wait()
    for stream in range(2):
        own_out_ref[stream, :, width:] = pack_lse(lses[2 * stream], lane)
        other_out_ref[stream, :, width:] = pack_lse(lses[2 * stream + 1], lane)


def attend(where, own, other, keys, values, stretch, wq, wv, bias, after):
    shards, _, shard_rows, padded = own.shape
    n = shards * shard_rows
    kn, width = keys.shape
    heads = width // HD
    out = jax.ShapeDtypeStruct((2, n, padded), BF16)
    return pl.pallas_call(
        attend_kernel,
        in_specs=[pl.BlockSpec(memory_space=pltpu.SMEM), VMEM, VMEM, HBM, HBM] + [VMEM] * 4 + [HBM],
        out_specs=[VMEM, VMEM],
        out_shape=[out, out],
        scratch_shapes=[pltpu.VMEM((kn, width), BF16)] * 2
        + [pltpu.VMEM((4 * n, kn), F32)] * 2
        + [pltpu.VMEM((4 * n, 128), F32)] * 4
        + [pltpu.SemaphoreType.DMA((2, heads))],
        cost_estimate=pl.CostEstimate(
            flops=16 * n * kn * heads * HD, bytes_accessed=4 * kn * width, transcendentals=4 * n * kn * heads
        ),
        compiler_params=small(51),
        name="attend",
    )(where, own, other, keys, values, stretch, wq, wv, bias, after)


def merge(pieces, width):
    lane = lax.broadcasted_iota(jnp.int32, (pieces[0].shape[0], 128), 1)
    lses = [unpack_lse(x[:, width:]) for x in pieces]
    best = lses[0]
    for lse in lses[1:]:
        best = jnp.maximum(best, lse)
    weights = [jnp.exp(lse - best) for lse in lses]
    total = weights[0]
    for w in weights[1:]:
        total = total + w
    weights = [w / total for w in weights]
    means = []
    for h in range(width // HD):
        at = h * HD
        mean = weights[0][:, h : h + 1] * pieces[0][:, at : at + HD].astype(F32)
        for w, x in zip(weights[1:], pieces[1:]):
            mean += w[:, h : h + 1] * x[:, at : at + HD].astype(F32)
        means.append(mean.astype(BF16))
    return means, pack_lse(best + jnp.log(total), lane)


def merge_pair_kernel(a_ref, b_ref, out_ref):
    width = out_ref.shape[2] - 128
    for s in range(2):
        means, lse = merge([a_ref[s], b_ref[s]], width)
        for h, mean in enumerate(means):
            out_ref[s, :, h * HD : (h + 1) * HD] = mean
        out_ref[s, :, width:] = lse


def merge_pair(a, b):
    return pl.pallas_call(
        merge_pair_kernel,
        in_specs=[VMEM, VMEM],
        out_specs=VMEM,
        compiler_params=small(),
        out_shape=jax.ShapeDtypeStruct(a.shape, BF16),
        cost_estimate=pl.CostEstimate(flops=8 * a.size, bytes_accessed=6 * a.size, transcendentals=0),
        name="merge_pair",
    )(a, b)


def merge_send_kernel(a_ref, b_ref, c_ref, out_ref):
    width = out_ref.shape[3] - 128
    for s in range(2):
        means, lse = merge([a_ref[s], b_ref[s], c_ref[s]], width)
        for at, block in enumerate(means + [lse]):
            for p in range(out_ref.shape[0]):
                out_ref[p, s, :, at * HD : (at + 1) * HD] = block[2 * p : 2 * p + 2]


def merge_send(a, b, c):
    _, n, padded = a.shape
    return pl.pallas_call(
        merge_send_kernel,
        in_specs=[VMEM, VMEM, VMEM],
        out_specs=VMEM,
        compiler_params=small(),
        out_shape=jax.ShapeDtypeStruct((n // 2, 2, 2, padded), BF16),
        cost_estimate=pl.CostEstimate(flops=12 * a.size, bytes_accessed=8 * a.size, transcendentals=0),
        name="merge_send",
    )(a, b, c)


def finish_kernel(x_ref, a_ref, b_ref):
    parts = x_ref.shape[0]
    groups, rows, width = a_ref.shape
    means, _ = merge([x_ref[z] for z in range(parts)], width)
    for h, mean in enumerate(means):
        for g in range(groups):
            at = 2 * rows * g
            a_ref[g, :, h * HD : (h + 1) * HD] = mean[at : at + rows]
            b_ref[g, :, h * HD : (h + 1) * HD] = mean[at + rows : at + 2 * rows]


def finish(x, groups, rows):
    out = jax.ShapeDtypeStruct((groups, rows, x.shape[2] - 128), BF16)
    return pl.pallas_call(
        finish_kernel, in_specs=[VMEM], out_specs=[VMEM, VMEM], out_shape=(out, out), compiler_params=small(), name="finish"
    )(x)


def local(
    response_input,
    response_queries,
    response_keys,
    response_values,
    prompt_keys,
    prompt_values,
    query_down_weight,
    query_up_weight,
    value_down_weight,
    value_up_weight,
    response_index,
):
    nz, ny, nc = (lax.axis_size(a) for a in ("z", "yh", "c"))
    groups = lax.axis_size("x") * lax.axis_size("yl")
    rows, model = response_queries.shape
    width = model // groups
    shard_rows = rows * groups
    side, core = lax.axis_index("yh"), lax.axis_index("c")
    part = (lax.axis_index("z") * ny + side) * nc + core
    group = lax.axis_index("x") * lax.axis_size("yl") + lax.axis_index("yl")

    def by_group(a):
        return a.reshape(rows, groups, width).transpose(1, 0, 2)

    padded = width + 128
    sent = prepare(
        response_input,
        by_group(response_queries),
        by_group(response_keys),
        by_group(response_values),
        query_down_weight.T,
        value_down_weight.T,
        ny,
    ).reshape(ny * groups, rows, 3 * width + 256)
    rows_in = lax.all_to_all(sent, ("yh", "x", "yl"), 0, 0, tiled=True).reshape(ny * shard_rows, 3 * width + 256)
    stretch = rows_in.reshape(ny, shard_rows, 3 * width + 256)
    own = lax.all_to_all(fan(rows_in, nz, padded), "z", 0, 0, tiled=True)
    other = lax.ppermute(own, "c", swap(nc))
    own = own.reshape(nz, ny, shard_rows, padded)
    other = other.reshape(nz, ny, shard_rows, padded)

    wq = lax.dynamic_slice_in_dim(query_up_weight, group * width, width, 1)
    wv = lax.dynamic_slice_in_dim(value_up_weight, group * width, width, 1)
    count = response_index.shape[0]
    key_pos = part * shard_rows + jnp.arange(shard_rows, dtype=jnp.int32)
    key_seg = lax.dynamic_slice_in_dim(response_index, part * shard_rows, shard_rows, 0)
    query_pos = jnp.arange(count, dtype=jnp.int32)
    seen = (key_pos[None, :] <= query_pos[:, None]) & (key_seg[None, :] == response_index[:, None])
    bias = jnp.where(seen, 0.0, HIDDEN).astype(F32)
    bias = bias.reshape(nz, ny * nc, shard_rows, shard_rows).transpose(1, 0, 2, 3)
    bias = bias.reshape(ny * nc, nz * shard_rows, shard_rows)

    def attend_side(far, after):
        to = side ^ far
        where = jnp.stack([to, 2 * to + core, 2 * to + 1 - core, side]).astype(jnp.int32)
        return attend(where, own, other, prompt_keys, prompt_values, stretch, wq, wv, bias, after)

    far_own, far_other = attend_side(1, own.reshape(2, nz * shard_rows, padded))
    far = merge_pair(far_own, lax.ppermute(far_other, "c", swap(nc)))
    crossed = lax.ppermute(far, "yh", swap(ny))
    near_own, near_other = attend_side(0, far)
    sends = merge_send(near_own, lax.ppermute(near_other, "c", swap(nc)), crossed)
    parts = lax.all_to_all(sends, ("z", "x", "yl"), 0, 0, tiled=True)
    outs = finish(parts.reshape(nz, groups * 2 * rows, padded), groups, rows)
    return tuple(o.transpose(1, 0, 2).reshape(rows, model) for o in outs)


def solution(mesh):
    axes = ("z", "yh", "c", "x", "yl")
    torus = Mesh(mesh.devices.reshape(8, 2, 2, 4, 2), axes)
    tokens = P(axes, None)
    cache = P(axes[:3], axes[3:])
    return jax.shard_map(
        local,
        mesh=torus,
        in_specs=(tokens,) * 4 + (cache,) * 2 + (P(),) * 5,
        out_specs=(tokens, tokens),
        check_vma=False,
    )
```

```python
import jax
import jax.numpy as jnp
from jax import lax
from jax.experimental import pallas as pl
from jax.experimental.pallas import tpu as pltpu
from jax.sharding import Mesh, PartitionSpec as P


HD = 128
SCALE = HD**-0.5
LOG2E = 1.4426950408889634
HIDDEN = -1e30
KEY_CHUNK = 512
LAST_DIMS = (((1,), (1,)), ((), ()))
BF16 = jnp.bfloat16
F32 = jnp.float32


def swap(size, flip=1):
    return [(i, i ^ flip) for i in range(size)]


VMEM = pl.BlockSpec(memory_space=pltpu.VMEM)
HBM = pl.BlockSpec(memory_space=pltpu.HBM)


FAR_MIB = 44
NEAR_MIB = 32


def small(limit=12):
    return pltpu.CompilerParams(vmem_limit_bytes=limit << 20)


def prepare_kernel(x_ref, q_ref, k_ref, v_ref, wq_ref, wv_ref, out_ref, f_ref):
    rank = wq_ref.shape[0]
    x = x_ref[...]
    f_ref[...] = jnp.zeros_like(f_ref)
    f_ref[0, :, :rank] = lax.dot_general(x, wq_ref[...], LAST_DIMS, preferred_element_type=F32)
    f_ref[1, :, :rank] = lax.dot_general(x, wv_ref[...], LAST_DIMS, preferred_element_type=F32)
    fq = f_ref[0].astype(BF16)
    fv = f_ref[1].astype(BF16)
    for g in range(q_ref.shape[0]):
        at = 0
        for piece in (q_ref[g], fq, k_ref[g], v_ref[g], fv):
            for half in range(out_ref.shape[0]):
                out_ref[half, g, :, at : at + piece.shape[1]] = piece
            at += piece.shape[1]


def prepare(x, q, k, v, wq, wv, halves):
    groups, rows, width = q.shape
    return pl.pallas_call(
        prepare_kernel,
        out_shape=jax.ShapeDtypeStruct((halves, groups, rows, 3 * width + 256), BF16),
        scratch_shapes=[pltpu.VMEM((2, rows, 128), F32)],
        name="prepare",
    )(x, q, k, v, wq, wv)


def pack_lse(lse, lane):
    lse = jnp.where(lane < 8, lse, 0.0)
    high = lse.astype(BF16).astype(F32)
    middle = (lse - high).astype(BF16).astype(F32)
    low = lse - high - middle
    return (high + pltpu.roll(middle, 8, 1) + pltpu.roll(low, 16, 1)).astype(BF16)


def unpack_lse(packed):
    x = packed.astype(F32)
    return x + pltpu.roll(x, 120, 1) + pltpu.roll(x, 112, 1)


def attend_far_kernel(
    where_ref, own_ref, other_ref, keys_hbm, values_hbm, stretch_ref, wq_ref, wv_ref, bias_ref,
    own_out_ref, other_out_ref, keys_ref, values_ref, *scratch,
):
    *scratch, sems = scratch

    def fetch(i, h):
        src, dst = ((keys_hbm, keys_ref), (values_hbm, values_ref))[i]
        cols = slice(h * HD, (h + 1) * HD)
        return pltpu.make_async_copy(src.at[:, cols], dst.at[:, cols], sems.at[i, h])

    heads = keys_ref.shape[1] // HD
    order = [(0, 0), (0, 1), (1, 0)] + [(i, h) for k in range(1, heads) for i, h in ((0, k + 1), (1, k)) if h < heads]
    for i, h in order:
        fetch(i, h).start()

    def arrive(step):
        cuts = (0, 1, 3, len(order))
        for i, h in order[cuts[step] : cuts[step + 1]] if step < 3 else ():
            fetch(i, h).wait()

    attend_body(
        0, where_ref, own_ref, other_ref, keys_ref, values_ref, stretch_ref, wq_ref, wv_ref, bias_ref,
        own_out_ref, other_out_ref, *scratch, arrive,
    )


def attend_near_kernel(
    where_ref, own_ref, other_ref, keys_ref, values_ref, stretch_ref, wq_ref, wv_ref, bias_ref, after_ref, *rest
):
    del after_ref
    attend_body(
        4, where_ref, own_ref, other_ref, keys_ref, values_ref, stretch_ref, wq_ref, wv_ref, bias_ref,
        *rest, lambda step: None,
    )


def attend_body(
    call, where_ref, own_ref, other_ref, keys_ref, values_ref, stretch_ref, wq_ref, wv_ref, bias_ref,
    own_out_ref, other_out_ref, s0_ref, s1_ref, m0_ref, m1_ref, o_ref, l_ref, arrive,
):
    side = where_ref[call]
    shards, _, shard_rows, _ = own_ref.shape
    n = shards * shard_rows
    rows = 4 * n
    kn, width = keys_ref.shape
    heads = width // HD
    rank = wq_ref.shape[0]
    scores_refs = (s0_ref, s1_ref)
    max_refs = (m0_ref, m1_ref)
    lane = lax.broadcasted_iota(jnp.int32, (n, 128), 1)
    bias_own = bias_ref[where_ref[call + 1]]
    bias_other = bias_ref[where_ref[call + 2]]
    keys_at = width + 128
    values_at = keys_at + width
    factors_at = values_at + width
    bias = jnp.concatenate([bias_own, bias_other, bias_own, bias_other], 0)

    def tokens(ref, at, size):
        return ref[:, side, :, at : at + size].reshape(n, size)

    factors = jnp.concatenate([tokens(own_ref, width, HD), tokens(other_ref, width, HD)], 0)[:, :rank]
    home = where_ref[call + 3]
    value_factors = stretch_ref[home, :, factors_at : factors_at + rank]

    def begin(h):
        at = h * HD
        base = jnp.concatenate([tokens(own_ref, at, HD), tokens(other_ref, at, HD)], 0)
        adapted = (
            base.astype(F32) + jnp.dot(factors, wq_ref[:, at : at + HD], preferred_element_type=F32)
        ).astype(BF16)
        q = jnp.concatenate([adapted, base], 0)
        near = lax.dot_general(q, stretch_ref[home, :, keys_at + at : keys_at + at + HD], LAST_DIMS, preferred_element_type=F32) + bias
        max_refs[h % 2][...] = jnp.broadcast_to(jnp.max(near, -1, keepdims=True), (rows, 128))
        return q, near

    def score(h, q, j):
        s = lax.dot_general(
            q, keys_ref[j : j + KEY_CHUNK, h * HD : (h + 1) * HD], LAST_DIMS, preferred_element_type=F32
        )
        scores_refs[h % 2][:, j : j + KEY_CHUNK] = s
        m = max_refs[h % 2][...]
        for c in range(0, KEY_CHUNK, 128):
            m = jnp.maximum(m, s[:, c : c + 128])
        max_refs[h % 2][...] = m

    q, near = begin(0)
    arrive(0)
    for j in range(0, kn, KEY_CHUNK):
        score(0, q, j)
    lses = [jnp.zeros((n, 128), F32) for _ in range(4)]
    for h in range(heads):
        at = h * HD
        arrive(h + 1)
        if h + 1 < heads:
            q, near_next = begin(h + 1)
        m = jnp.max(max_refs[h % 2][...], -1, keepdims=True)
        near_probs = jnp.exp2((near - m) * (SCALE * LOG2E))
        near_total = jnp.sum(near_probs, -1, keepdims=True)
        near_probs = near_probs.astype(BF16)
        base_values = stretch_ref[home, :, values_at + at : values_at + at + HD]
        adapted_values = (
            base_values.astype(F32) + jnp.dot(value_factors, wv_ref[:, at : at + HD], preferred_element_type=F32)
        ).astype(BF16)
        o_ref[: 2 * n] = jnp.dot(near_probs[: 2 * n], adapted_values, preferred_element_type=F32)
        o_ref[2 * n :] = jnp.dot(near_probs[2 * n :], base_values, preferred_element_type=F32)
        l_ref[...] = jnp.zeros_like(l_ref)
        for j in range(0, kn, KEY_CHUNK):
            if h + 1 < heads:
                score(h + 1, q, j)
            p = jnp.exp2((scores_refs[h % 2][:, j : j + KEY_CHUNK] - m) * (SCALE * LOG2E))
            total = l_ref[...]
            for c in range(0, KEY_CHUNK, 128):
                total += p[:, c : c + 128]
            l_ref[...] = total
            o_ref[...] += jnp.dot(
                p.astype(BF16), values_ref[j : j + KEY_CHUNK, at : at + HD], preferred_element_type=F32
            )
        total = jnp.sum(l_ref[...], -1, keepdims=True) + near_total
        mean = (o_ref[...] / total).astype(BF16)
        lse = m * SCALE + jnp.log(total)
        for stream in range(2):
            for partner, out_ref in enumerate((own_out_ref, other_out_ref)):
                i = 2 * stream + partner
                out_ref[stream, :, at : at + HD] = mean[i * n : (i + 1) * n]
                lses[i] = jnp.where(lane == h, lse[i * n : (i + 1) * n], lses[i])
        if h + 1 < heads:
            near = near_next
    for stream in range(2):
        own_out_ref[stream, :, width:] = pack_lse(lses[2 * stream], lane)
        other_out_ref[stream, :, width:] = pack_lse(lses[2 * stream + 1], lane)


def attend(where, own, other, keys, values, stretch, wq, wv, bias, after=None):
    shards, _, shard_rows, padded = own.shape
    n = shards * shard_rows
    kn, width = keys.shape
    heads = width // HD
    out = jax.ShapeDtypeStruct((2, n, padded), BF16)
    cache = jax.ShapeDtypeStruct((kn, width), BF16)
    far = after is None
    scratch = [pltpu.VMEM((4 * n, kn), F32)] * 2 + [pltpu.VMEM((4 * n, 128), F32)] * 4
    smem = pl.BlockSpec(memory_space=pltpu.SMEM)
    return pl.pallas_call(
        attend_far_kernel if far else attend_near_kernel,
        in_specs=[smem, VMEM, VMEM] + [HBM if far else VMEM] * 2 + [VMEM] * 4 + [HBM] * (not far),
        out_specs=[VMEM] * (4 if far else 2),
        out_shape=[out, out] + [cache, cache] * far,
        scratch_shapes=scratch + [pltpu.SemaphoreType.DMA((2, heads))] * far,
        cost_estimate=pl.CostEstimate(
            flops=16 * n * kn * heads * HD, bytes_accessed=4 * kn * width, transcendentals=4 * n * kn * heads
        ),
        compiler_params=small(FAR_MIB if far else NEAR_MIB),
        name="attend_far" if far else "attend_near",
    )(where, own, other, keys, values, stretch, wq, wv, bias, *(() if far else (after,)))


def merge(pieces, width):
    lane = lax.broadcasted_iota(jnp.int32, (pieces[0].shape[0], 128), 1)
    lses = [unpack_lse(x[:, width:]) for x in pieces]
    best = lses[0]
    for lse in lses[1:]:
        best = jnp.maximum(best, lse)
    weights = [jnp.exp(lse - best) for lse in lses]
    total = weights[0]
    for w in weights[1:]:
        total = total + w
    weights = [w / total for w in weights]
    means = []
    for h in range(width // HD):
        at = h * HD
        mean = weights[0][:, h : h + 1] * pieces[0][:, at : at + HD].astype(F32)
        for w, x in zip(weights[1:], pieces[1:]):
            mean += w[:, h : h + 1] * x[:, at : at + HD].astype(F32)
        means.append(mean.astype(BF16))
    return means, pack_lse(best + jnp.log(total), lane)


def merge_pair_kernel(a_ref, b_ref, out_ref):
    width = out_ref.shape[2] - 128
    for s in range(2):
        means, lse = merge([a_ref[s], b_ref[s]], width)
        for h, mean in enumerate(means):
            out_ref[s, :, h * HD : (h + 1) * HD] = mean
        out_ref[s, :, width:] = lse


def merge_pair(a, b):
    return pl.pallas_call(
        merge_pair_kernel,
        in_specs=[VMEM, VMEM],
        out_specs=VMEM,
        compiler_params=small(),
        out_shape=jax.ShapeDtypeStruct(a.shape, BF16),
        cost_estimate=pl.CostEstimate(flops=8 * a.size, bytes_accessed=6 * a.size, transcendentals=0),
        name="merge_pair",
    )(a, b)


def merge_send_kernel(a_ref, b_ref, c_ref, out_ref):
    width = out_ref.shape[3] - 128
    for s in range(2):
        means, lse = merge([a_ref[s], b_ref[s], c_ref[s]], width)
        for at, block in enumerate(means + [lse]):
            for p in range(out_ref.shape[0]):
                out_ref[p, s, :, at * HD : (at + 1) * HD] = block[2 * p : 2 * p + 2]


def merge_send(a, b, c):
    _, n, padded = a.shape
    return pl.pallas_call(
        merge_send_kernel,
        in_specs=[VMEM, VMEM, VMEM],
        out_specs=VMEM,
        compiler_params=small(),
        out_shape=jax.ShapeDtypeStruct((n // 2, 2, 2, padded), BF16),
        cost_estimate=pl.CostEstimate(flops=12 * a.size, bytes_accessed=8 * a.size, transcendentals=0),
        name="merge_send",
    )(a, b, c)


def finish_kernel(x_ref, a_ref, b_ref):
    parts = x_ref.shape[0]
    groups, rows, width = a_ref.shape
    means, _ = merge([x_ref[z] for z in range(parts)], width)
    for h, mean in enumerate(means):
        for g in range(groups):
            at = 2 * rows * g
            a_ref[g, :, h * HD : (h + 1) * HD] = mean[at : at + rows]
            b_ref[g, :, h * HD : (h + 1) * HD] = mean[at + rows : at + 2 * rows]


def finish(x, groups, rows):
    out = jax.ShapeDtypeStruct((groups, rows, x.shape[2] - 128), BF16)
    return pl.pallas_call(
        finish_kernel, in_specs=[VMEM], out_specs=[VMEM, VMEM], out_shape=(out, out), compiler_params=small(), name="finish"
    )(x)


def local(
    response_input,
    response_queries,
    response_keys,
    response_values,
    prompt_keys,
    prompt_values,
    query_down_weight,
    query_up_weight,
    value_down_weight,
    value_up_weight,
    response_index,
):
    nz, ny, nc = (lax.axis_size(a) for a in ("z", "yh", "c"))
    groups = lax.axis_size("x") * lax.axis_size("yl")
    rows, model = response_queries.shape
    width = model // groups
    shard_rows = rows * groups
    side, core = lax.axis_index("yh"), lax.axis_index("c")
    part = (lax.axis_index("z") * ny + side) * nc + core
    group = lax.axis_index("x") * lax.axis_size("yl") + lax.axis_index("yl")

    def by_group(a):
        return a.reshape(rows, groups, width).transpose(1, 0, 2)

    padded = width + 128
    sent = prepare(
        response_input,
        by_group(response_queries),
        by_group(response_keys),
        by_group(response_values),
        query_down_weight.T,
        value_down_weight.T,
        ny,
    ).reshape(ny * groups, rows, 3 * width + 256)
    rows_in = lax.all_to_all(sent, ("yh", "x", "yl"), 0, 0, tiled=True).reshape(ny * shard_rows, 3 * width + 256)
    stretch = rows_in.reshape(ny, shard_rows, 3 * width + 256)
    copies = jnp.broadcast_to(rows_in[None, :, :padded], (nz, ny * shard_rows, padded))
    own = lax.all_to_all(copies, "z", 0, 0, tiled=True)
    other = lax.ppermute(own, "c", swap(nc))
    own = own.reshape(nz, ny, shard_rows, padded)
    other = other.reshape(nz, ny, shard_rows, padded)

    wq = lax.dynamic_slice_in_dim(query_up_weight, group * width, width, 1)
    wv = lax.dynamic_slice_in_dim(value_up_weight, group * width, width, 1)
    count = response_index.shape[0]
    key_pos = part * shard_rows + jnp.arange(shard_rows, dtype=jnp.int32)
    key_seg = lax.dynamic_slice_in_dim(response_index, part * shard_rows, shard_rows, 0)
    query_pos = jnp.arange(count, dtype=jnp.int32)
    seen = (key_pos[None, :] <= query_pos[:, None]) & (key_seg[None, :] == response_index[:, None])
    bias = jnp.where(seen, 0.0, HIDDEN).astype(F32)
    bias = bias.reshape(nz, ny * nc, shard_rows, shard_rows).transpose(1, 0, 2, 3)
    bias = bias.reshape(ny * nc, nz * shard_rows, shard_rows)

    where = []
    for to in (1 - side, side):
        where += [to, 2 * to + core, 2 * to + 1 - core, side]
    where = jnp.stack(where).astype(jnp.int32)
    far_own, far_other, keys, values = attend(
        where, own, other, prompt_keys, prompt_values, stretch, wq, wv, bias
    )
    far = merge_pair(far_own, lax.ppermute(far_other, "c", swap(nc)))
    crossed = lax.ppermute(far, "yh", swap(ny))
    near_own, near_other = attend(where, own, other, keys, values, stretch, wq, wv, bias, far)
    sends = merge_send(near_own, lax.ppermute(near_other, "c", swap(nc)), crossed)
    parts = lax.all_to_all(sends, ("z", "x", "yl"), 0, 0, tiled=True)
    outs = finish(parts.reshape(nz, groups * 2 * rows, padded), groups, rows)
    return tuple(o.transpose(1, 0, 2).reshape(rows, model) for o in outs)


def solution(mesh):
    axes = ("z", "yh", "c", "x", "yl")
    torus = Mesh(mesh.devices.reshape(8, 2, 2, 4, 2), axes)
    tokens = P(axes, None)
    cache = P(axes[:3], axes[3:])
    return jax.shard_map(
        local,
        mesh=torus,
        in_specs=(tokens,) * 4 + (cache,) * 2 + (P(),) * 5,
        out_specs=(tokens, tokens),
        check_vma=False,
    )
```
